1024 devices in a mesh: ens: 16 (over y_lo, x, core), polar: 64 (over z, y_hi).
Axes of the slice: x: 4, y: 8 (y_hi: 4, y_lo: 2; y = y_hi * 2 + y_lo), z: 16, core: 2. Of those that a mesh axis runs over, the one named last changes fastest.
Arguments:
- field: bfloat16 [16, 384, 96, 720], P('ens', 'polar'), may hold values from -6 to 6
- target: bfloat16 [384, 384, 720], P('polar'), may hold values from -6 to 6
- slot_orders: int32 [384], replicated, may hold values from 0 to 383, each once
- analysis: bfloat16 [384, 384, 360], P('polar'), may hold values from -0.3125 to 0.3125
- synthesis: bfloat16 [384, 360, 384], P('polar'), may hold values from -0.3125 to 0.3125
- degree_filter: float32 [384, 360], replicated, may hold values from -4 to 4
Outputs:
- prediction: bfloat16 [16, 384, 96, 720], P('ens', 'polar')
- gradient: bfloat16 [16, 384, 96, 720], P('ens', 'polar')
The draws below stay inside these ranges and needn't reach their ends.
Inputs may be any that keep to these rules, and one draw needn't show every extreme that they name: `slot_orders`: each slot number 0 to 383 appears once; a slot whose order is 360 or more is empty.
All inputs are finite; a program needn't handle non-finite values.
Results may differ from the reference program's by a relative error of at most 0.006.
Values may be sent and summed in bfloat16 or wider, within the bound.
No kernel may reach another device: no remote copies, remote signals or barrier semaphores. Data moves between devices by JAX's collectives and lax.ppermute only.
A program may use at most 64 MiB of HBM per device.

```python
import math
import jax
import jax.numpy as jnp
from jax import lax

NLON = 720
MAX_DEGREE = 360
CW = 96
ENS = 4
C = 384
LATITUDE_COUNT = 384
ORDER_SLOTS = 384
N_ENS = 16


def block_scale(key, extent, cuts, least, high):
    def one(position, shards_of):
        draws = jax.random.uniform(jax.random.fold_in(jax.random.fold_in(key, 6), position), (shards_of,), jnp.float32, least / len(cuts), high / len(cuts))
        return jnp.repeat(jnp.exp(draws), extent[position] // shards_of).reshape((-1,) + (1,) * (len(extent) - position - 1))

    loudness = one(*cuts[0])
    for cut in cuts[1:]:
        loudness = loudness * one(*cut)
    return loudness


def centred(own_key, dims, deviation, bound, shards=(), kind=jnp.bfloat16):
    loudness = block_scale(own_key, dims, shards, -0.22, 0.18) if shards else 1.0
    array = jax.random.normal(own_key, dims, jnp.float32) * deviation * loudness
    return jnp.minimum(jnp.maximum(array, -bound), bound).astype(kind)


def setup_inputs(seed: int = 0) -> dict:
    arg_keys = jax.random.split(jax.random.key(seed), 7)
    return {
        "field": centred(arg_keys[0], (N_ENS, LATITUDE_COUNT, CW, NLON), 1.0, 6.0, ((0, 16), (1, 64))),
        "target": centred(arg_keys[1], (LATITUDE_COUNT, C, NLON), 1.0, 6.0, ((0, 64),)),
        "slot_orders": jax.random.permutation(arg_keys[2], ORDER_SLOTS).astype(jnp.int32),
        "analysis": centred(arg_keys[3], (ORDER_SLOTS, LATITUDE_COUNT, MAX_DEGREE), LATITUDE_COUNT ** -0.5, 0.3125, ((0, 64),)),
        "synthesis": centred(arg_keys[4], (ORDER_SLOTS, MAX_DEGREE, LATITUDE_COUNT), MAX_DEGREE ** -0.5, 0.3125, ((0, 64),)),
        "degree_filter": centred(arg_keys[5], (C, MAX_DEGREE), 1.0, 4.0, (), jnp.float32),
    }


smooth_sq = 0.25

def lon_tables(slot_orders, lon_count, degree_total):
    orders = slot_orders.astype(jnp.int32)
    points = jnp.arange(lon_count, dtype=jnp.int32)
    phase = orders[:, None] * points[None, :] % lon_count
    angle = phase.astype(jnp.float32) * (2.0 * math.pi / lon_count)
    live = (orders < degree_total).astype(jnp.float32)[:, None]
    cosine = jnp.cos(angle) * live
    sine = jnp.sin(angle) * live
    paired = jnp.stack([cosine, -sine], 1)
    forward = (paired / math.sqrt(lon_count)).astype(jnp.bfloat16)
    inverse = (paired / math.sqrt(degree_total)).astype(jnp.bfloat16)
    return (forward, inverse)

def kernel_slope(diff):
    return diff / jnp.sqrt(diff * diff + smooth_sq)

def reference(field, target, slot_orders, analysis, synthesis, degree_filter):
    slab_count, lat_count, chan_count, lon_count = field.shape
    group_count = slab_count // ENS
    slot_count, degree_total = (analysis.shape[0], analysis.shape[2])
    forward, inverse = lon_tables(slot_orders, lon_count, degree_total)
    degrees = jnp.arange(degree_total, dtype=jnp.int32)
    keeping = (degrees[None, :] >= slot_orders.astype(jnp.int32)[:, None]).astype(jnp.float32)
    filters = degree_filter.astype(jnp.float32).reshape(group_count, chan_count, degree_total)
    slab_weights = jnp.repeat(filters, ENS, axis=0)
    flat_forward = forward.reshape(slot_count * 2, lon_count).T

    def one_member(inputs):
        member, rows = inputs
        scaling = rows[None, None] * keeping[:, None, None, :]
        flat = member.reshape(lat_count * chan_count, lon_count)
        spectral = jnp.dot(flat, flat_forward, preferred_element_type=jnp.float32).astype(jnp.bfloat16)
        spectral = spectral.reshape(lat_count, chan_count, slot_count, 2).transpose(2, 3, 1, 0)
        coeffs = jnp.einsum('spct,stl->spcl', spectral.astype(jnp.float32), analysis.astype(jnp.float32))
        scaled = (coeffs * scaling).astype(jnp.bfloat16)
        bands = jnp.einsum('spcl,slt->spct', scaled.astype(jnp.float32), synthesis.astype(jnp.float32)).astype(jnp.bfloat16)
        synth = jnp.einsum('spct,spk->tck', bands.astype(jnp.float32), inverse.astype(jnp.float32))
        return (member.astype(jnp.float32) + synth).astype(jnp.bfloat16)
    prediction = lax.map(one_member, (field, slab_weights))

    def per_cycle(inputs):
        members, observed = inputs
        values = members.astype(jnp.float32)
        own_term = kernel_slope(values - observed.astype(jnp.float32)[None])

        def add_member(summed, other):
            return (summed + kernel_slope(values - other[None]), None)
        pair_sum, unused = lax.scan(add_member, jnp.zeros_like(values), values)
        return (own_term - pair_sum / ENS).astype(jnp.bfloat16)
    grouped = prediction.reshape(group_count, ENS, lat_count, chan_count, lon_count)
    grouped = grouped.transpose(0, 2, 1, 3, 4).reshape(group_count * lat_count, ENS, chan_count, lon_count)
    observed = target.reshape(lat_count, group_count, chan_count, lon_count).transpose(1, 0, 2, 3)
    observed = observed.reshape(group_count * lat_count, chan_count, lon_count)
    slopes = lax.map(per_cycle, (grouped, observed))
    slopes = slopes.reshape(group_count, lat_count, ENS, chan_count, lon_count).transpose(0, 2, 1, 3, 4)
    gradient = slopes.reshape(slab_count, lat_count, chan_count, lon_count)
    return (prediction, gradient)
```

```python
import functools
import math

import jax
import jax.numpy as jnp
from jax import lax
from jax.experimental import pallas as pl
from jax.experimental.pallas import tpu as pltpu
from jax.sharding import PartitionSpec as P

ENS = 4
BF = jnp.bfloat16
F32 = jnp.float32
smooth_sq = 0.25
LANES = 128


def turn_sine(turns):
    w = turns * (2.0 * math.pi)
    w2 = w * w
    poly = -2.5052108e-8 + w2 * 1.6059044e-10
    for coef in (2.7557319e-6, -1.9841270e-4, 8.3333333e-3, -1.6666667e-1, 1.0):
        poly = poly * w2 + coef
    return poly * w


def cosine_sine(orders, points, lon_count):
    product = orders * points
    phase = product - jnp.floor(product * (1.0 / lon_count)) * lon_count
    turns = phase * (1.0 / lon_count)
    cosine = turn_sine(jnp.abs(turns - 0.5) - 0.25)
    shifted = turns + 0.75
    shifted = jnp.where(shifted >= 1.0, shifted - 1.0, shifted)
    sine = turn_sine(jnp.abs(shifted - 0.5) - 0.25)
    return cosine, sine


def fill_table(orders_ref, table_ref, lon_count, degree_total, scale):
    bands, mine = orders_ref.shape
    steps = -(-lon_count // LANES)
    lane = lax.broadcasted_iota(jnp.int32, (bands, LANES), 1).astype(F32)
    for s in range(mine):
        order = orders_ref[:, s : s + 1].astype(F32)
        gain = jnp.where(order < degree_total, scale, 0.0)
        fc, fs = cosine_sine(jnp.broadcast_to(order, lane.shape), lane, lon_count)
        fc, fs = fc * gain, fs * gain
        cc, cs = cosine_sine(jnp.broadcast_to(order, lane.shape), lane * LANES, lon_count)
        low = 2 * s * bands
        for j in range(steps):
            width = min(LANES, lon_count - j * LANES)
            c, q = cc[:, j : j + 1], cs[:, j : j + 1]
            cosine = fc * c - fs * q
            sine = fs * c + fc * q
            span = slice(j * LANES, j * LANES + width)
            table_ref[low : low + bands, span] = cosine[:, :width].astype(BF)
            table_ref[low + bands : low + 2 * bands, span] = (-sine[:, :width]).astype(BF)


def analyse_kernel(orders_ref, field_ref, out_ref, table, rows, *, degree_total, lon_count):
    lat, chan, lon = field_ref.shape
    bands, mine = orders_ref.shape
    pieces = 2 * mine
    fill_table(orders_ref, table, lon_count, degree_total, 1.0 / math.sqrt(lon_count))
    for t in range(lat):
        got = lax.dot_general(
            table[...], field_ref[t], (((1,), (1,)), ((), ())), preferred_element_type=F32
        )
        for half in range(0, pieces, 4):
            line = jnp.concatenate(
                [got[j * bands : (j + 1) * bands] for j in range(half, half + 4)], 1
            )
            for q in range(4 * chan // LANES):
                tile = half * chan // LANES + q
                rows[tile, pl.ds(t, bands, lat), :] = line[:, q * LANES : (q + 1) * LANES]
    for q in range(rows.shape[0]):
        out_ref[:, q * LANES : (q + 1) * LANES] = rows[q].astype(BF)


def analyse(orders, field, degree_total):
    lat, chan, lon = field.shape
    bands, mine = orders.shape
    return pl.pallas_call(
        functools.partial(analyse_kernel, degree_total=degree_total, lon_count=lon),
        out_shape=jax.ShapeDtypeStruct((bands * lat, 2 * mine * chan), BF),
        scratch_shapes=[
            pltpu.VMEM((2 * mine * bands, lon), BF),
            pltpu.VMEM((2 * mine * chan // LANES, bands * lat, LANES), F32),
        ],
        name="analyse",
    )(orders, field)


def table_kernel(orders_ref, out_ref, *, degree_total, lon_count):
    fill_table(orders_ref, out_ref, lon_count, degree_total, 1.0 / math.sqrt(degree_total))


def inverse_table(orders, lon_count, degree_total):
    bands, mine = orders.shape
    return pl.pallas_call(
        functools.partial(table_kernel, degree_total=degree_total, lon_count=lon_count),
        out_shape=jax.ShapeDtypeStruct((2 * mine * bands, lon_count), BF),
        name="inverse_table",
    )(orders)


def legendre_kernel(mine_ref, x_ref, a_ref, s_ref, filter_ref, out_ref):
    chan = filter_ref.shape[1]
    degree = lax.broadcasted_iota(jnp.int32, filter_ref.shape, 0)
    outs = []
    for h in range(2):
        order = mine_ref[2 * pl.program_id(0) + h]
        gain = jnp.where(degree >= order, filter_ref[...], 0.0)
        gain = jnp.concatenate([gain, gain], 1)
        x = x_ref[:, 2 * chan * h : 2 * chan * (h + 1)]
        coeffs = jnp.dot(a_ref[h], x, preferred_element_type=F32)
        scaled = (coeffs * gain).astype(BF)
        outs.append(
            lax.dot_general(s_ref[h], scaled, (((0,), (0,)), ((), ())), preferred_element_type=F32)
        )
    out_ref[...] = jnp.concatenate(outs, 1).astype(BF)


def legendre(mine, x, a, s, filters):
    slots, degrees, lat_all = a.shape
    chan = filters.shape[1]
    step = 2
    wide = pl.BlockSpec((lat_all, step * 2 * chan), lambda i, m: (0, i))
    table = pl.BlockSpec((step, degrees, lat_all), lambda i, m: (i, 0, 0))
    return pl.pallas_call(
        legendre_kernel,
        grid_spec=pltpu.PrefetchScalarGridSpec(
            num_scalar_prefetch=1,
            grid=(slots // step,),
            in_specs=[wide, table, table, pl.BlockSpec((degrees, chan), lambda i, m: (0, 0))],
            out_specs=wide,
        ),
        out_shape=jax.ShapeDtypeStruct(x.shape, BF),
        name="legendre",
    )(mine, x, a, s, filters)


def synth_kernel(table_ref, x_ref, field_ref, out_ref, rows, cols):
    lat, chan, lon = field_ref.shape
    pieces = x_ref.shape[1] // chan
    bands = x_ref.shape[0] // lat
    tiles = rows.shape[0]
    for q in range(tiles):
        rows[q] = x_ref[:, q * LANES : (q + 1) * LANES].astype(F32)
    for t in range(lat):
        line = jnp.concatenate([rows[q, pl.ds(t, bands, lat), :] for q in range(tiles)], 1).astype(BF)
        for j in range(pieces):
            cols[j * bands : (j + 1) * bands, :] = line[:, j * chan : (j + 1) * chan]
        total = lax.dot_general(
            cols[...], table_ref[...], (((0,), (0,)), ((), ())), preferred_element_type=F32
        )
        out_ref[t] = (field_ref[t].astype(F32) + total).astype(BF)


def synthesise(table, x, field):
    lat, chan, lon = field.shape
    return pl.pallas_call(
        synth_kernel,
        out_shape=jax.ShapeDtypeStruct(field.shape, BF),
        scratch_shapes=[
            pltpu.VMEM((x.shape[1] // LANES, x.shape[0], LANES), F32),
            pltpu.VMEM((table.shape[0], chan), BF),
        ],
        name="synthesise",
    )(table, x, field)


def crps_kernel(own_ref, a_ref, b_ref, c_ref, seen_ref, out_ref):
    own = own_ref[...].astype(F32)

    def slope(other):
        d = own - other.astype(F32)
        return d * lax.rsqrt(d * d + smooth_sq)

    pair = slope(a_ref[...]) + slope(b_ref[...]) + slope(c_ref[...])
    out_ref[...] = (slope(seen_ref[...]) - pair * (1.0 / ENS)).astype(BF)


def crps(own, a, b, c, seen):
    lat, chan, lon = own.shape
    spec = pl.BlockSpec((1, chan, lon), lambda t: (t, 0, 0))
    return pl.pallas_call(
        crps_kernel,
        grid=(lat,),
        in_specs=[spec] * 5,
        out_specs=spec,
        out_shape=jax.ShapeDtypeStruct(own.shape, BF),
        name="crps",
    )(own, a, b, c, seen)


def body(field, target, slot_orders, analysis, synthesis, degree_filter):
    lat, chan, lon = field.shape[1:]
    mine_count, degrees = analysis.shape[0], analysis.shape[2]
    bands = lax.axis_size("polar")
    ens = lax.axis_size("ens")
    width = 2 * mine_count * chan
    packed = (bands, lat // 2, 2, width)
    orders = slot_orders.reshape(bands, mine_count)
    spectral = analyse(orders, field[0], degrees).reshape(packed)
    got = lax.all_to_all(spectral, "polar", split_axis=0, concat_axis=0, tiled=True)
    inverse = inverse_table(orders, lon, degrees)
    group = lax.axis_index("ens") // ENS
    pick = (group * chan + jnp.arange(chan)[:, None] == jnp.arange(target.shape[1])[None, :]).astype(BF)
    seen = jnp.einsum("qc,tck->tqk", pick, target, preferred_element_type=F32).astype(BF)
    mine = lax.dynamic_slice_in_dim(slot_orders, lax.axis_index("polar") * mine_count, mine_count)
    filters = lax.dynamic_slice_in_dim(degree_filter.T, group * chan, chan, 1)
    out = legendre(
        mine, got.reshape(bands * lat, width), jnp.swapaxes(analysis, 1, 2), synthesis, filters
    )
    back = lax.all_to_all(out.reshape(packed), "polar", split_axis=0, concat_axis=0, tiled=True)
    prediction = synthesise(inverse, back.reshape(bands * lat, width), field[0])
    across = [(i, i ^ 2) for i in range(ens)]
    beside = [(i, i ^ 1) for i in range(ens)]
    parts = []
    half = lat // 2
    for h in range(2):
        own = prediction[h * half : (h + 1) * half]
        far = lax.ppermute(own, "ens", across)
        near = lax.ppermute(own, "ens", beside)
        far_near = lax.ppermute(far, "ens", beside)
        parts.append(crps(own, near, far, far_near, seen[h * half : (h + 1) * half]))
    gradient = jnp.concatenate(parts, 0)
    return prediction[None], gradient[None]


def solution(mesh):
    in_specs = (
        P("ens", "polar", None, None),
        P("polar", None, None),
        P(),
        P("polar", None, None),
        P("polar", None, None),
        P(),
    )
    out_specs = (P("ens", "polar", None, None), P("ens", "polar", None, None))
    return jax.shard_map(body, mesh=mesh, in_specs=in_specs, out_specs=out_specs, check_vma=False)
```

```python
import functools
import math

import jax
import jax.numpy as jnp
from jax import lax
from jax.experimental import pallas as pl
from jax.experimental.pallas import tpu as pltpu
from jax.sharding import PartitionSpec as P

ENS = 4
BF = jnp.bfloat16
F32 = jnp.float32
smooth_sq = 0.25
LANES = 128
GROUP = 2


def turn_sine(turns):
    w = turns * (2.0 * math.pi)
    w2 = w * w
    poly = -2.5052108e-8 + w2 * 1.6059044e-10
    for coef in (2.7557319e-6, -1.9841270e-4, 8.3333333e-3, -1.6666667e-1, 1.0):
        poly = poly * w2 + coef
    return poly * w


def cosine_sine(orders, points, lon_count):
    product = orders * points
    phase = product - jnp.floor(product * (1.0 / lon_count)) * lon_count
    turns = phase * (1.0 / lon_count)
    cosine = turn_sine(jnp.abs(turns - 0.5) - 0.25)
    shifted = turns + 0.75
    shifted = jnp.where(shifted >= 1.0, shifted - 1.0, shifted)
    sine = turn_sine(jnp.abs(shifted - 0.5) - 0.25)
    return cosine, sine


def fill_table(orders_ref, table_ref, bands, lon_count, degree_total, scale):
    slots = orders_ref.shape[1]
    mine = slots // bands
    shape = (bands, LANES)
    lane = lax.broadcasted_iota(jnp.int32, shape, 1).astype(F32)
    every = orders_ref[...].astype(F32)
    first = mine * lax.broadcasted_iota(jnp.int32, (bands, slots), 0)
    place = lax.broadcasted_iota(jnp.int32, (bands, slots), 1)
    for s in range(mine):
        order = jnp.sum(jnp.where(place == first + s, every, 0.0), 1, keepdims=True)
        order = jnp.broadcast_to(order, shape)
        gain = jnp.where(order < degree_total, scale, 0.0)
        cosine, sine = cosine_sine(order, lane, lon_count)
        cosine, sine = cosine * gain, sine * gain
        turn_c, turn_s = cosine_sine(order, float(LANES), lon_count)
        low = 2 * s * bands
        for start in range(0, lon_count, LANES):
            width = min(LANES, lon_count - start)
            span = slice(start, start + width)
            table_ref[low : low + bands, span] = cosine[:, :width].astype(BF)
            table_ref[low + bands : low + 2 * bands, span] = (-sine[:, :width]).astype(BF)
            cosine, sine = cosine * turn_c - sine * turn_s, sine * turn_c + cosine * turn_s


def analyse_kernel(orders_ref, field_ref, out_ref, table, rows, *, bands, degree_total):
    lat, chan, lon = field_ref.shape
    pieces = table.shape[0] // bands
    fill_table(orders_ref, table, bands, lon, degree_total, 1.0 / math.sqrt(lon))
    group = GROUP
    for t0 in range(0, lat, group):
        got = lax.dot_general(
            table[...],
            field_ref[t0 : t0 + group].reshape(group * chan, lon),
            (((1,), (1,)), ((), ())),
            preferred_element_type=F32,
        )
        for u in range(group):
            for start in range(0, pieces, 4):
                line = jnp.concatenate(
                    [
                        got[j * bands : (j + 1) * bands, u * chan : (u + 1) * chan]
                        for j in range(start, start + 4)
                    ],
                    1,
                )
                for q in range(4 * chan // LANES):
                    tile = start * chan // LANES + q
                    rows[tile, pl.ds(t0 + u, bands, lat), :] = line[:, q * LANES : (q + 1) * LANES]
    for q in range(rows.shape[0]):
        packed = rows[q].astype(BF).reshape(out_ref.shape[0], 2, LANES)
        out_ref[:, :, q * LANES : (q + 1) * LANES] = packed


def analyse(orders, field, bands, degree_total):
    lat, chan, lon = field.shape
    pieces = 2 * orders.shape[1] // bands
    return pl.pallas_call(
        functools.partial(analyse_kernel, bands=bands, degree_total=degree_total),
        out_shape=jax.ShapeDtypeStruct((bands * lat // 2, 2, pieces * chan), BF),
        scratch_shapes=[
            pltpu.VMEM((pieces * bands, lon), BF),
            pltpu.VMEM((pieces * chan // LANES, bands * lat, LANES), F32),
        ],
        name="analyse",
    )(orders, field)


def table_kernel(orders_ref, out_ref, *, bands, degree_total):
    scale = 1.0 / math.sqrt(degree_total)
    fill_table(orders_ref, out_ref, bands, out_ref.shape[1], degree_total, scale)


def inverse_table(orders, bands, lon_count, degree_total):
    return pl.pallas_call(
        functools.partial(table_kernel, bands=bands, degree_total=degree_total),
        out_shape=jax.ShapeDtypeStruct((2 * orders.shape[1], lon_count), BF),
        name="inverse_table",
    )(orders)


def legendre_kernel(mine_ref, x_ref, a_ref, s_ref, filter_ref, out_ref):
    chan = filter_ref.shape[1]
    lat_all = a_ref.shape[2]
    degree = lax.broadcasted_iota(jnp.int32, filter_ref.shape, 0)
    both = x_ref[...].reshape(lat_all, x_ref.shape[2])
    outs = []
    for h in range(2):
        order = mine_ref[2 * pl.program_id(0) + h]
        gain = jnp.where(degree >= order, filter_ref[...], 0.0)
        gain = jnp.concatenate([gain, gain], 1)
        x = both[:, 2 * chan * h : 2 * chan * (h + 1)]
        coeffs = jnp.dot(a_ref[h], x, preferred_element_type=F32)
        scaled = (coeffs * gain).astype(BF)
        outs.append(jnp.dot(s_ref[h], scaled, preferred_element_type=F32))
    out_ref[...] = jnp.concatenate(outs, 1).astype(BF).reshape(out_ref.shape)


def legendre(mine, x, a, s, filters):
    slots, degrees, lat_all = a.shape
    chan = filters.shape[1]
    step = 2
    wide = pl.BlockSpec((lat_all // 2, 2, step * 2 * chan), lambda i, m: (0, 0, i))
    return pl.pallas_call(
        legendre_kernel,
        grid_spec=pltpu.PrefetchScalarGridSpec(
            num_scalar_prefetch=1,
            grid=(slots // step,),
            in_specs=[
                wide,
                pl.BlockSpec((step, degrees, lat_all), lambda i, m: (i, 0, 0)),
                pl.BlockSpec((step, lat_all, degrees), lambda i, m: (i, 0, 0)),
                pl.BlockSpec((degrees, chan), lambda i, m: (0, 0)),
            ],
            out_specs=wide,
        ),
        out_shape=jax.ShapeDtypeStruct(x.shape, BF),
        name="legendre",
    )(mine, x, a, s, filters)


def synth_kernel(table_ref, x_ref, field_ref, out_ref, low_ref, high_ref, rows, cols):
    lat, chan, lon = field_ref.shape
    pieces = x_ref.shape[2] // chan
    bands = table_ref.shape[0] // pieces
    tiles = rows.shape[0]
    first = low_ref.shape[0]
    for q in range(tiles):
        rows[q] = x_ref[:, :, q * LANES : (q + 1) * LANES].reshape(lat * bands, LANES).astype(F32)
    for t in range(lat):
        line = jnp.concatenate([rows[q, pl.ds(t, bands, lat), :] for q in range(tiles)], 1).astype(BF)
        for j in range(pieces):
            cols[j * bands : (j + 1) * bands, :] = line[:, j * chan : (j + 1) * chan]
        total = lax.dot_general(
            cols[...], table_ref[...], (((0,), (0,)), ((), ())), preferred_element_type=F32
        )
        done = (field_ref[t].astype(F32) + total).astype(BF)
        out_ref[t] = done
        if t < first:
            low_ref[t] = done
        else:
            high_ref[t - first] = done


def synthesise(table, x, field, first):
    lat, chan, lon = field.shape
    tiles = x.shape[2] // LANES
    return pl.pallas_call(
        synth_kernel,
        out_shape=[
            jax.ShapeDtypeStruct((n, chan, lon), BF) for n in (lat, first, lat - first)
        ],
        scratch_shapes=[
            pltpu.VMEM((tiles, x.shape[0] * 2, LANES), F32),
            pltpu.VMEM((table.shape[0], chan), BF),
        ],
        name="synthesise",
    )(table, x, field)


def crps_kernel(own_ref, near_ref, far_ref, far_near_ref, seen_ref, *rest):
    out_ref = rest[-1]
    own = own_ref[...].astype(F32)

    def slope(other):
        d = own - other[...].astype(F32)
        return d * lax.rsqrt(d * d + smooth_sq)

    pair = slope(near_ref) + slope(far_ref) + slope(far_near_ref)
    out_ref[...] = (slope(seen_ref) - pair * (1.0 / ENS)).astype(BF)


def crps(own, near, far, far_near, seen, start, filled=None):
    lat, chan, lon = near.shape
    part = pl.BlockSpec((1, chan, lon), lambda t: (t, 0, 0))
    whole = pl.BlockSpec((1, chan, lon), lambda t: (t + start, 0, 0))
    more = [] if filled is None else [filled]
    return pl.pallas_call(
        crps_kernel,
        grid=(lat,),
        in_specs=[whole, part, part, part, whole] + [pl.BlockSpec(memory_space=pl.ANY)] * len(more),
        out_specs=whole,
        out_shape=jax.ShapeDtypeStruct(own.shape, BF),
        input_output_aliases={5: 0} if more else {},
        name="crps",
    )(own, near, far, far_near, seen, *more)


def body(field, target, slot_orders, analysis, synthesis, degree_filter):
    lat, chan, lon = field.shape[1:]
    mine_count, degrees = analysis.shape[0], analysis.shape[2]
    bands = lax.axis_size("polar")
    ens = lax.axis_size("ens")
    width = 2 * mine_count * chan
    packed = (bands, lat // 2, 2, width)
    flat = (bands * lat // 2, 2, width)
    orders = slot_orders.reshape(1, bands * mine_count)
    spectral = analyse(orders, field[0], bands, degrees).reshape(packed)
    got = lax.all_to_all(spectral, "polar", split_axis=0, concat_axis=0, tiled=True)
    group = lax.axis_index("ens") // ENS
    mine = lax.dynamic_slice_in_dim(slot_orders, lax.axis_index("polar") * mine_count, mine_count)
    filters = lax.dynamic_slice_in_dim(degree_filter.T, group * chan, chan, 1)
    turned = jnp.swapaxes(synthesis, 1, 2)
    got, turned, filters = lax.optimization_barrier((got, turned, filters))
    out = legendre(mine, got.reshape(flat), jnp.swapaxes(analysis, 1, 2), turned, filters)
    back = lax.all_to_all(out.reshape(packed), "polar", split_axis=0, concat_axis=0, tiled=True)
    inverse = inverse_table(orders, bands, lon, degrees)
    pick = (group * chan + jnp.arange(chan)[:, None] == jnp.arange(target.shape[1])[None, :]).astype(BF)
    seen = jnp.einsum("qc,tck->tqk", pick, target, preferred_element_type=F32).astype(BF)
    back, inverse, seen = lax.optimization_barrier((back, inverse, seen))
    first = 4
    prediction, low, high = synthesise(inverse, back.reshape(flat), field[0], first)
    across = [(i, i ^ 2) for i in range(ens)]
    beside = [(i, i ^ 1) for i in range(ens)]
    gradient = None
    for start, own in ((0, low), (first, high)):
        far = lax.ppermute(own, "ens", across)
        near = lax.ppermute(own, "ens", beside)
        far_near = lax.ppermute(far, "ens", beside)
        gradient = crps(prediction, near, far, far_near, seen, start, gradient)
    return prediction[None], gradient[None]


def solution(mesh):
    in_specs = (
        P("ens", "polar", None, None),
        P("polar", None, None),
        P(),
        P("polar", None, None),
        P("polar", None, None),
        P(),
    )
    out_specs = (P("ens", "polar", None, None), P("ens", "polar", None, None))
    return jax.shard_map(body, mesh=mesh, in_specs=in_specs, out_specs=out_specs, check_vma=False)
```

```python
import functools
import math

import jax
import jax.numpy as jnp
from jax import lax
from jax.experimental import pallas as pl
from jax.experimental.pallas import tpu as pltpu
from jax.sharding import PartitionSpec as P


ENS = 4
BF = jnp.bfloat16
F32 = jnp.float32
smooth_sq = 0.25
LANES = 128
CHUNKS = 3
GROUP = 2


def turn_sine(turns):
    w = turns * (2.0 * math.pi)
    w2 = w * w
    poly = -2.5052108e-8 + w2 * 1.6059044e-10
    for coef in (2.7557319e-6, -1.9841270e-4, 8.3333333e-3, -1.6666667e-1, 1.0):
        poly = poly * w2 + coef
    return poly * w


def cosine_sine(orders, points, lon_count):
    product = orders * points
    phase = product - jnp.floor(product * (1.0 / lon_count)) * lon_count
    turns = phase * (1.0 / lon_count)
    cosine = turn_sine(jnp.abs(turns - 0.5) - 0.25)
    shifted = turns + 0.75
    shifted = jnp.where(shifted >= 1.0, shifted - 1.0, shifted)
    sine = turn_sine(jnp.abs(shifted - 0.5) - 0.25)
    return cosine, sine


def fill_table(orders_ref, table_ref, bands, lon_count, degree_total, scale):
    slots = orders_ref.shape[0]
    mine = slots // bands
    shape = (bands, LANES)
    lane = lax.broadcasted_iota(jnp.int32, shape, 1).astype(F32)
    every = orders_ref[...].reshape(1, slots).astype(F32)
    first = mine * lax.broadcasted_iota(jnp.int32, (bands, slots), 0)
    place = lax.broadcasted_iota(jnp.int32, (bands, slots), 1)
    for s in range(mine):
        order = jnp.sum(jnp.where(place == first + s, every, 0.0), 1, keepdims=True)
        order = jnp.broadcast_to(order, shape)
        gain = jnp.where(order < degree_total, scale, 0.0)
        cosine, sine = cosine_sine(order, lane, lon_count)
        cosine, sine = cosine * gain, sine * gain
        turn_c, turn_s = cosine_sine(order, float(LANES), lon_count)
        low = 2 * s * bands
        for start in range(0, lon_count, LANES):
            width = min(LANES, lon_count - start)
            span = slice(start, start + width)
            table_ref[low : low + bands, span] = cosine[:, :width].astype(BF)
            table_ref[low + bands : low + 2 * bands, span] = (-sine[:, :width]).astype(BF)
            cosine, sine = cosine * turn_c - sine * turn_s, sine * turn_c + cosine * turn_s


def analyse_kernel(orders_ref, field_ref, out_ref, table, rows, *, bands, degree_total):
    lat, chan, lon = field_ref.shape
    pieces = table.shape[0] // bands
    fill_table(orders_ref, table, bands, lon, degree_total, 1.0 / math.sqrt(lon))
    group = GROUP
    for t0 in range(0, lat, group):
        got = lax.dot_general(
            table[...],
            field_ref[t0 : t0 + group].reshape(group * chan, lon),
            (((1,), (1,)), ((), ())),
            preferred_element_type=F32,
        )
        for u in range(group):
            for start in range(0, pieces, 4):
                line = jnp.concatenate(
                    [
                        got[j * bands : (j + 1) * bands, u * chan : (u + 1) * chan]
                        for j in range(start, start + 4)
                    ],
                    1,
                )
                for q in range(4 * chan // LANES):
                    tile = start * chan // LANES + q
                    rows[tile, pl.ds(t0 + u, bands, lat), :] = line[:, q * LANES : (q + 1) * LANES]
    for q in range(rows.shape[0]):
        packed = rows[q].astype(BF).reshape(out_ref.shape[0], 2, LANES)
        out_ref[:, :, q * LANES : (q + 1) * LANES] = packed


def analyse(orders, field, bands, degree_total):
    lat, chan, lon = field.shape
    pieces = 2 * orders.shape[0] // bands
    return pl.pallas_call(
        functools.partial(analyse_kernel, bands=bands, degree_total=degree_total),
        out_shape=jax.ShapeDtypeStruct((bands * lat // 2, 2, pieces * chan), BF),
        scratch_shapes=[
            pltpu.VMEM((pieces * bands, lon), BF),
            pltpu.VMEM((pieces * chan // LANES, bands * lat, LANES), F32),
        ],
        name="analyse",
    )(orders, field)


def table_kernel(orders_ref, out_ref, *, bands, degree_total):
    scale = 1.0 / math.sqrt(degree_total)
    fill_table(orders_ref, out_ref, bands, out_ref.shape[1], degree_total, scale)


def inverse_table(orders, bands, lon_count, degree_total):
    return pl.pallas_call(
        functools.partial(table_kernel, bands=bands, degree_total=degree_total),
        out_shape=jax.ShapeDtypeStruct((2 * orders.shape[0], lon_count), BF),
        name="inverse_table",
    )(orders)


def legendre_kernel(mine_ref, x_ref, a_ref, s_ref, filter_ref, out_ref):
    chan = filter_ref.shape[1]
    lat_all = a_ref.shape[2]
    degree = lax.broadcasted_iota(jnp.int32, filter_ref.shape, 0)
    both = x_ref[...].reshape(lat_all, x_ref.shape[2])
    outs = []
    for h in range(2):
        order = mine_ref[2 * pl.program_id(0) + h]
        gain = jnp.where(degree >= order, filter_ref[...], 0.0)
        gain = jnp.concatenate([gain, gain], 1)
        x = both[:, 2 * chan * h : 2 * chan * (h + 1)]
        coeffs = jnp.dot(a_ref[h], x, preferred_element_type=F32)
        scaled = (coeffs * gain).astype(BF)
        outs.append(jnp.dot(s_ref[h], scaled, preferred_element_type=F32))
    out_ref[...] = jnp.concatenate(outs, 1).astype(BF).reshape(out_ref.shape)


def legendre(mine, x, a, s, filters):
    slots, degrees, lat_all = a.shape
    chan = filters.shape[1]
    step = 2
    wide = pl.BlockSpec((lat_all // 2, 2, step * 2 * chan), lambda i, m: (0, 0, i))
    return pl.pallas_call(
        legendre_kernel,
        grid_spec=pltpu.PrefetchScalarGridSpec(
            num_scalar_prefetch=1,
            grid=(slots // step,),
            in_specs=[
                wide,
                pl.BlockSpec((step, degrees, lat_all), lambda i, m: (i, 0, 0)),
                pl.BlockSpec((step, lat_all, degrees), lambda i, m: (i, 0, 0)),
                pl.BlockSpec((degrees, chan), lambda i, m: (0, 0)),
            ],
            out_specs=wide,
        ),
        out_shape=jax.ShapeDtypeStruct(x.shape, BF),
        name="legendre",
    )(mine, x, a, s, filters)


def synth_kernel(table_ref, x_ref, field_ref, *rest):
    out_ref, part_ref, rows, cols = rest[-4:]
    count, chan, _ = field_ref.shape
    bands = x_ref.shape[0]
    pieces = table_ref.shape[0] // bands
    tiles = rows.shape[0]
    for q in range(tiles):
        tile = x_ref[:, 0, :, q * LANES : (q + 1) * LANES]
        rows[q] = tile.reshape(count * bands, LANES).astype(F32)
    for t in range(count):
        line = [rows[q, pl.ds(t, bands, count), :] for q in range(tiles)]
        line = jnp.concatenate(line, 1).astype(BF)
        for j in range(pieces):
            piece = line[:, j * chan : (j + 1) * chan]
            cols[j * bands : (j + 1) * bands, t * chan : (t + 1) * chan] = piece
    total = lax.dot_general(
        cols[...], table_ref[...], (((0,), (0,)), ((), ())), preferred_element_type=F32
    )
    for t in range(count):
        done = (field_ref[t].astype(F32) + total[t * chan : (t + 1) * chan]).astype(BF)
        out_ref[t] = done
        part_ref[t] = done


def synthesise(table, x, field, place, filled=None):
    _, chan, lon = field.shape
    bands, _, count, width = x.shape
    tiles = width // LANES
    block = pl.BlockSpec((count, chan, lon), lambda i: (place, 0, 0))
    more = [] if filled is None else [filled]
    return pl.pallas_call(
        synth_kernel,
        grid=(1,),
        in_specs=[
            pl.BlockSpec(table.shape, lambda i: (0, 0)),
            pl.BlockSpec((bands, 1, count, width), lambda i: (0, place, 0, 0)),
            block,
        ]
        + [pl.BlockSpec(memory_space=pl.ANY)] * len(more),
        out_specs=[block, pl.BlockSpec((count, chan, lon), lambda i: (0, 0, 0))],
        out_shape=[
            jax.ShapeDtypeStruct(field.shape, BF),
            jax.ShapeDtypeStruct((count, chan, lon), BF),
        ],
        input_output_aliases={3: 0} if more else {},
        scratch_shapes=[
            pltpu.VMEM((tiles, count * bands, LANES), F32),
            pltpu.VMEM((table.shape[0], count * chan), BF),
        ],
        name="synthesise",
    )(table, x, field, *more)


def crps_kernel(own_ref, near_ref, far_ref, far_near_ref, seen_ref, *rest):
    out_ref = rest[-1]
    own = own_ref[...].astype(F32)

    def slope(other):
        d = own - other[...].astype(F32)
        return d * lax.rsqrt(d * d + smooth_sq)

    pair = slope(near_ref) + slope(far_ref) + slope(far_near_ref)
    out_ref[...] = (slope(seen_ref) - pair * (1.0 / ENS)).astype(BF)


def crps(own, near, far, far_near, seen, start, filled=None):
    lat, chan, lon = far.shape
    part = pl.BlockSpec((1, chan, lon), lambda t: (t, 0, 0))
    whole = pl.BlockSpec((1, chan, lon), lambda t: (t + start, 0, 0))
    more = [] if filled is None else [filled]
    return pl.pallas_call(
        crps_kernel,
        grid=(lat,),
        in_specs=[whole, whole, part, part, whole] + [pl.BlockSpec(memory_space=pl.ANY)] * len(more),
        out_specs=whole,
        out_shape=jax.ShapeDtypeStruct(own.shape, BF),
        input_output_aliases={5: 0} if more else {},
        name="crps",
    )(own, near, far, far_near, seen, *more)


def body(field, target, slot_orders, analysis, synthesis, degree_filter):
    lat, chan, lon = field.shape[1:]
    mine_count, degrees = analysis.shape[0], analysis.shape[2]
    bands = lax.axis_size("polar")
    ens = lax.axis_size("ens")
    width = 2 * mine_count * chan
    packed = (bands, lat // 2, 2, width)
    flat = (bands * lat // 2, 2, width)
    spectral = analyse(slot_orders, field[0], bands, degrees).reshape(packed)
    got = lax.all_to_all(spectral, "polar", split_axis=0, concat_axis=0, tiled=True)
    group = lax.axis_index("ens") // ENS
    mine = lax.dynamic_slice_in_dim(slot_orders, lax.axis_index("polar") * mine_count, mine_count)
    filters = lax.dynamic_slice_in_dim(degree_filter.T, group * chan, chan, 1)
    turned = jnp.swapaxes(synthesis, 1, 2)
    got, turned, filters = lax.optimization_barrier((got, turned, filters))
    out = legendre(mine, got.reshape(flat), jnp.swapaxes(analysis, 1, 2), turned, filters)
    back = lax.all_to_all(out.reshape(packed), "polar", split_axis=0, concat_axis=0, tiled=True)
    inverse = inverse_table(slot_orders, bands, lon, degrees)
    pick = (group * chan + jnp.arange(chan)[:, None] == jnp.arange(target.shape[1])[None, :]).astype(BF)
    seen = jnp.einsum("qc,tck->tqk", pick, target, preferred_element_type=F32).astype(BF)
    back, inverse, seen = lax.optimization_barrier((back, inverse, seen))
    across = [(i, i ^ 2) for i in range(ens)]
    beside = [(i, i ^ 1) for i in range(ens)]
    count = 2
    prediction = gradient = None
    fars = []
    for k in range(CHUNKS):
        prediction, part = synthesise(
            inverse, back, field[0], k, prediction
        )
        fars.append(lax.ppermute(part, "ens", across))
    near = lax.ppermute(prediction, "ens", beside)
    for k, far in enumerate(fars):
        far_near = lax.ppermute(far, "ens", beside)
        gradient = crps(prediction, near, far, far_near, seen, k * count, gradient)
    return prediction[None], gradient[None]


def solution(mesh):
    in_specs = (
        P("ens", "polar", None, None),
        P("polar", None, None),
        P(),
        P("polar", None, None),
        P("polar", None, None),
        P(),
    )
    out_specs = (P("ens", "polar", None, None), P("ens", "polar", None, None))
    return jax.shard_map(body, mesh=mesh, in_specs=in_specs, out_specs=out_specs, check_vma=False)
```

```python
import functools
import math

import jax
import jax.numpy as jnp
from jax import lax
from jax.experimental import pallas as pl
from jax.experimental.pallas import tpu as pltpu
from jax.sharding import PartitionSpec as P


ENS = 4
BF = jnp.bfloat16
F32 = jnp.float32
smooth_sq = 0.25
LANES = 128
CHUNKS = 3
VMEM = pl.BlockSpec(memory_space=pltpu.VMEM)
LIMIT = pltpu.CompilerParams(vmem_limit_bytes=20 << 20)


def on_chip(*arrays):
    return [pltpu.with_memory_space_constraint(a, pltpu.VMEM) for a in arrays]


def off_chip(*arrays):
    return [pltpu.with_memory_space_constraint(a, pltpu.HBM) for a in arrays]


GROUP = 2


def turn_sine(turns):
    w = turns * (2.0 * math.pi)
    w2 = w * w
    poly = -2.5052108e-8 + w2 * 1.6059044e-10
    for coef in (2.7557319e-6, -1.9841270e-4, 8.3333333e-3, -1.6666667e-1, 1.0):
        poly = poly * w2 + coef
    return poly * w


def cosine_sine(orders, points, lon_count):
    product = orders * points
    phase = product - jnp.floor(product * (1.0 / lon_count)) * lon_count
    turns = phase * (1.0 / lon_count)
    cosine = turn_sine(jnp.abs(turns - 0.5) - 0.25)
    shifted = turns + 0.75
    shifted = jnp.where(shifted >= 1.0, shifted - 1.0, shifted)
    sine = turn_sine(jnp.abs(shifted - 0.5) - 0.25)
    return cosine, sine


def fill_table(orders_ref, table_ref, bands, lon_count, degree_total, scale):
    slots = orders_ref.shape[0]
    mine = slots // bands
    shape = (bands, LANES)
    lane = lax.broadcasted_iota(jnp.int32, shape, 1).astype(F32)
    every = orders_ref[...].reshape(1, slots).astype(F32)
    first = mine * lax.broadcasted_iota(jnp.int32, (bands, slots), 0)
    place = lax.broadcasted_iota(jnp.int32, (bands, slots), 1)
    for s in range(mine):
        order = jnp.sum(jnp.where(place == first + s, every, 0.0), 1, keepdims=True)
        order = jnp.broadcast_to(order, shape)
        gain = jnp.where(order < degree_total, scale, 0.0)
        cosine, sine = cosine_sine(order, lane, lon_count)
        cosine, sine = cosine * gain, sine * gain
        turn_c, turn_s = cosine_sine(order, float(LANES), lon_count)
        low = 2 * s * bands
        for start in range(0, lon_count, LANES):
            width = min(LANES, lon_count - start)
            span = slice(start, start + width)
            table_ref[low : low + bands, span] = cosine[:, :width].astype(BF)
            table_ref[low + bands : low + 2 * bands, span] = (-sine[:, :width]).astype(BF)
            cosine, sine = cosine * turn_c - sine * turn_s, sine * turn_c + cosine * turn_s


def send(source, sink, sems, part, width):
    span = pl.ds(part * width, width)
    return pltpu.make_async_copy(source.at[:, :, span], sink.at[:, :, span], sems.at[part])


def analyse_kernel(orders_ref, source_ref, sink_ref, field_ref, out_ref, table, rows, sem, sent, *, bands, degree_total):
    lat, chan, lon = field_ref.shape
    pieces = table.shape[0] // bands
    copy = pltpu.make_async_copy(source_ref, field_ref, sem)
    copy.start()
    fill_table(orders_ref, table, bands, lon, degree_total, 1.0 / math.sqrt(lon))
    copy.wait()
    group = GROUP
    for t0 in range(0, lat, group):
        got = lax.dot_general(
            table[...],
            field_ref[t0 : t0 + group].reshape(group * chan, lon),
            (((1,), (1,)), ((), ())),
            preferred_element_type=F32,
        )
        for u in range(group):
            for start in range(0, pieces, 4):
                line = jnp.concatenate(
                    [
                        got[j * bands : (j + 1) * bands, u * chan : (u + 1) * chan]
                        for j in range(start, start + 4)
                    ],
                    1,
                )
                for q in range(4 * chan // LANES):
                    tile = start * chan // LANES + q
                    rows[tile, pl.ds(t0 + u, bands, lat), :] = line[:, q * LANES : (q + 1) * LANES]
    for q in range(rows.shape[0]):
        packed = rows[q].astype(BF).reshape(out_ref.shape[0], 2, LANES)
        out_ref[:, :, q * LANES : (q + 1) * LANES] = packed
        if q % 3 == 2:
            send(out_ref, sink_ref, sent, q // 3, 3 * LANES).start()
    for g in range(3):
        send(out_ref, sink_ref, sent, g, 3 * LANES).wait()


def analyse(orders, field, bands, degree_total):
    lat, chan, lon = field.shape
    pieces = 2 * orders.shape[0] // bands
    return pl.pallas_call(
        functools.partial(analyse_kernel, bands=bands, degree_total=degree_total),
        in_specs=[VMEM, pl.BlockSpec(memory_space=pl.ANY)],
        out_specs=pl.BlockSpec(memory_space=pl.ANY),
        out_shape=pltpu.HBM((bands * lat // 2, 2, pieces * chan), BF),
        scratch_shapes=[
            pltpu.VMEM(field.shape, BF),
            pltpu.VMEM((bands * lat // 2, 2, pieces * chan), BF),
            pltpu.VMEM((pieces * bands, lon), BF),
            pltpu.VMEM((pieces * chan // LANES, bands * lat, LANES), F32),
            pltpu.SemaphoreType.DMA,
            pltpu.SemaphoreType.DMA((3,)),
        ],
        compiler_params=LIMIT,
        name="analyse",
    )(orders, *off_chip(field))


def tables_kernel(group_ref, a_ref, s_ref, filter_ref, a_out, s_out, filter_out, sem):
    chan = filter_out.shape[1]
    copy = pltpu.make_async_copy(a_ref, a_out, sem)
    copy.start()
    for i in range(s_ref.shape[0]):
        s_out[i] = s_ref[i].astype(F32).T.astype(BF)
    group = group_ref[0]
    kept = filter_ref[:, :chan]
    for g in range(1, filter_ref.shape[1] // chan):
        kept = jnp.where(group == g, filter_ref[:, g * chan : (g + 1) * chan], kept)
    filter_out[...] = kept
    copy.wait()


def tables(group, a, s, filters, chan):
    slots, degrees, lat_all = a.shape
    return pl.pallas_call(
        tables_kernel,
        in_specs=[
            pl.BlockSpec(memory_space=pltpu.SMEM),
            pl.BlockSpec(memory_space=pl.ANY),
            VMEM,
            VMEM,
        ],
        out_specs=[VMEM] * 3,
        out_shape=[
            pltpu.VMEM(a.shape, BF),
            pltpu.HBM((slots, lat_all, degrees), BF),
            pltpu.VMEM((degrees, chan), F32),
        ],
        scratch_shapes=[pltpu.SemaphoreType.DMA],
        compiler_params=LIMIT,
        name="tables",
    )(group, *off_chip(a, s, filters))


def scene_kernel(
    group_ref, orders_ref, target_ref, source_ref, table_out, seen_out, field_out, sem, *, bands, degree_total
):
    lat, chan, lon = field_out.shape
    copy = pltpu.make_async_copy(source_ref, field_out, sem)
    copy.start()
    fill_table(orders_ref, table_out, bands, lon, degree_total, 1.0 / math.sqrt(degree_total))
    shape = (chan, target_ref.shape[2])
    place = lax.broadcasted_iota(jnp.int32, shape, 1) - group_ref[0] * chan
    pick = jnp.where(place == lax.broadcasted_iota(jnp.int32, shape, 0), 1.0, 0.0).astype(BF)
    for t in range(lat):
        seen = lax.dot_general(
            pick, target_ref[t], (((1,), (1,)), ((), ())), preferred_element_type=F32
        )
        seen_out[t] = seen.astype(BF)
    copy.wait()


def scene(group, orders, target, field, bands, degree_total):
    _, _, lon = field.shape
    return pl.pallas_call(
        functools.partial(scene_kernel, bands=bands, degree_total=degree_total),
        in_specs=[
            pl.BlockSpec(memory_space=pltpu.SMEM),
            VMEM,
            VMEM,
            pl.BlockSpec(memory_space=pl.ANY),
        ],
        out_specs=[VMEM] * 3,
        out_shape=[
            pltpu.VMEM((2 * orders.shape[0], lon), BF),
            pltpu.HBM(field.shape, BF),
            pltpu.VMEM(field.shape, BF),
        ],
        scratch_shapes=[pltpu.SemaphoreType.DMA],
        compiler_params=LIMIT,
        name="scene",
    )(group, orders, *off_chip(target, field))


def legendre_kernel(
    mine_ref, x_ref, a_ref, source_ref, filter_ref, sink_ref, s_ref, out_ref, come, sent
):
    slots, _, lat_all = a_ref.shape
    copies = [
        pltpu.make_async_copy(source_ref.at[i], s_ref.at[i], come.at[i]) for i in range(slots)
    ]
    for copy in copies:
        copy.start()
    chan = filter_ref.shape[1]
    degree = lax.broadcasted_iota(jnp.int32, filter_ref.shape, 0)
    for g in range(slots // 2):
        span = slice(g * 4 * chan, (g + 1) * 4 * chan)
        both = x_ref[:, :, span].reshape(lat_all, 4 * chan)
        outs = []
        for h in range(2):
            gain = jnp.where(degree >= mine_ref[2 * g + h], filter_ref[...], 0.0)
            gain = jnp.concatenate([gain, gain], 1)
            x = both[:, 2 * chan * h : 2 * chan * (h + 1)]
            coeffs = jnp.dot(a_ref[2 * g + h], x, preferred_element_type=F32)
            scaled = (coeffs * gain).astype(BF)
            copies[2 * g + h].wait()
            outs.append(jnp.dot(s_ref[2 * g + h], scaled, preferred_element_type=F32))
        out_ref[:, :, span] = jnp.concatenate(outs, 1).astype(BF).reshape(lat_all // 2, 2, 4 * chan)
        send(out_ref, sink_ref, sent, g, 4 * chan).start()
    for g in range(slots // 2):
        send(out_ref, sink_ref, sent, g, 4 * chan).wait()


def legendre(mine, x, a, s, filters):
    return pl.pallas_call(
        legendre_kernel,
        in_specs=[
            pl.BlockSpec(memory_space=pltpu.SMEM),
            VMEM,
            VMEM,
            pl.BlockSpec(memory_space=pl.ANY),
            VMEM,
        ],
        out_specs=pl.BlockSpec(memory_space=pl.ANY),
        out_shape=pltpu.HBM(x.shape, BF),
        scratch_shapes=[
            pltpu.VMEM(s.shape, BF),
            pltpu.VMEM(x.shape, BF),
            pltpu.SemaphoreType.DMA((s.shape[0],)),
            pltpu.SemaphoreType.DMA((s.shape[0] // 2,)),
        ],
        compiler_params=LIMIT,
        name="legendre",
    )(mine, *on_chip(x, a), *off_chip(s), *on_chip(filters))


def synth_kernel(table_ref, x_ref, field_ref, *rest, place):
    out_ref, part_ref, rows, cols = rest[-4:]
    count, chan, _ = part_ref.shape
    bands = x_ref.shape[0]
    pieces = table_ref.shape[0] // bands
    tiles = rows.shape[0]
    for q in range(tiles):
        tile = x_ref[:, place, :, q * LANES : (q + 1) * LANES]
        rows[q] = tile.reshape(count * bands, LANES).astype(F32)
    for t in range(count):
        line = [rows[q, pl.ds(t, bands, count), :] for q in range(tiles)]
        line = jnp.concatenate(line, 1).astype(BF)
        for j in range(pieces):
            piece = line[:, j * chan : (j + 1) * chan]
            cols[j * bands : (j + 1) * bands, t * chan : (t + 1) * chan] = piece
    total = lax.dot_general(
        cols[...], table_ref[...], (((0,), (0,)), ((), ())), preferred_element_type=F32
    )
    for t in range(count):
        at = place * count + t
        done = (field_ref[at].astype(F32) + total[t * chan : (t + 1) * chan]).astype(BF)
        out_ref[at] = done
        part_ref[t] = done


def synthesise(table, x, field, place, filled=None):
    _, chan, lon = field.shape
    bands, _, count, width = x.shape
    tiles = width // LANES
    more = [] if filled is None else [filled]
    return pl.pallas_call(
        functools.partial(synth_kernel, place=place),
        in_specs=[VMEM] * (3 + len(more)),
        out_specs=[VMEM, VMEM],
        out_shape=[pltpu.VMEM(field.shape, BF), pltpu.VMEM((count, chan, lon), BF)],
        input_output_aliases={3: 0} if more else {},
        scratch_shapes=[
            pltpu.VMEM((tiles, count * bands, LANES), F32),
            pltpu.VMEM((table.shape[0], count * chan), BF),
        ],
        compiler_params=LIMIT,
        name="synthesise",
    )(*on_chip(table, x, field, *more))


def crps_kernel(own_ref, near_ref, far_ref, far_near_ref, seen_ref, *rest, start):
    out_ref = rest[-1]
    t = pl.program_id(0)
    own = own_ref[start + t].astype(F32)

    def slope(other):
        d = own - other.astype(F32)
        return d * lax.rsqrt(d * d + smooth_sq)

    pair = slope(near_ref[start + t]) + slope(far_ref[t]) + slope(far_near_ref[t])
    out_ref[0] = (slope(seen_ref[start + t]) - pair * (1.0 / ENS)).astype(BF)


def crps(own, near, far, far_near, seen, start, filled=None):
    lat, chan, lon = far.shape
    more = [] if filled is None else [filled]
    return pl.pallas_call(
        functools.partial(crps_kernel, start=start),
        grid=(lat,),
        in_specs=[VMEM] * 5 + [pl.BlockSpec(memory_space=pl.ANY)] * len(more),
        out_specs=pl.BlockSpec((1, chan, lon), lambda t: (t + start, 0, 0)),
        out_shape=jax.ShapeDtypeStruct(own.shape, BF),
        input_output_aliases={5: 0} if more else {},
        compiler_params=LIMIT,
        name="crps",
    )(*on_chip(own, near, far, far_near, seen), *more)


def body(field, target, slot_orders, analysis, synthesis, degree_filter):
    lat, chan, _ = field.shape[1:]
    mine_count, degrees = analysis.shape[0], analysis.shape[2]
    bands = lax.axis_size("polar")
    ens = lax.axis_size("ens")
    width = 2 * mine_count * chan
    packed = (bands, lat // 2, 2, width)
    flat = (bands * lat // 2, 2, width)
    spectral = analyse(slot_orders, field[0], bands, degrees).reshape(packed)
    got = lax.all_to_all(spectral, "polar", split_axis=0, concat_axis=0, tiled=True)
    group = (lax.axis_index("ens") // ENS).reshape(1)
    mine = lax.dynamic_slice_in_dim(slot_orders, lax.axis_index("polar") * mine_count, mine_count)
    ready = tables(group, jnp.swapaxes(analysis, 1, 2), synthesis, degree_filter.T, chan)
    got, mine, *ready = lax.optimization_barrier((got, mine, *ready))
    out = legendre(mine, got.reshape(flat), *ready)
    back = lax.all_to_all(out.reshape(packed), "polar", split_axis=0, concat_axis=0, tiled=True)
    ready = scene(group, slot_orders, jnp.swapaxes(target, 1, 2), field[0], bands, degrees)
    back, inverse, seen, near_field = lax.optimization_barrier((back, *ready))
    across = [(i, i ^ 2) for i in range(ens)]
    beside = [(i, i ^ 1) for i in range(ens)]
    count = 2
    prediction = gradient = None
    fars = []
    for k in range(CHUNKS):
        prediction, part = synthesise(
            inverse, back, near_field, k, prediction
        )
        fars.append(lax.ppermute(part, "ens", across))
    near = lax.ppermute(prediction, "ens", beside)
    for k, far in enumerate(fars):
        far_near = lax.ppermute(far, "ens", beside)
        gradient = crps(prediction, near, far, far_near, seen, k * count, gradient)
    return prediction[None], gradient[None]


def solution(mesh):
    in_specs = (
        P("ens", "polar", None, None),
        P("polar", None, None),
        P(),
        P("polar", None, None),
        P("polar", None, None),
        P(),
    )
    out_specs = (P("ens", "polar", None, None), P("ens", "polar", None, None))
    return jax.shard_map(body, mesh=mesh, in_specs=in_specs, out_specs=out_specs, check_vma=False)
```

```python
import functools
import math

import jax
import jax.numpy as jnp
from jax import lax
from jax.experimental import pallas as pl
from jax.experimental.pallas import tpu as pltpu
from jax.sharding import PartitionSpec as P


ENS = 4
BF = jnp.bfloat16
F32 = jnp.float32
smooth_sq = 0.25
LANES = 128
CHUNKS = ((0,), (1,), (2,))
HELD = 2
VMEM = pl.BlockSpec(memory_space=pltpu.VMEM)
LIMIT = pltpu.CompilerParams(vmem_limit_bytes=20 << 20)


def on_chip(*arrays):
    return [pltpu.with_memory_space_constraint(a, pltpu.VMEM) for a in arrays]


def off_chip(*arrays):
    return [pltpu.with_memory_space_constraint(a, pltpu.HBM) for a in arrays]


GROUP = 2


def turn_sine(turns):
    w = turns * (2.0 * math.pi)
    w2 = w * w
    poly = -2.5052108e-8 + w2 * 1.6059044e-10
    for coef in (2.7557319e-6, -1.9841270e-4, 8.3333333e-3, -1.6666667e-1, 1.0):
        poly = poly * w2 + coef
    return poly * w


def cosine_sine(orders, points, lon_count):
    product = orders * points
    phase = product - jnp.floor(product * (1.0 / lon_count)) * lon_count
    turns = phase * (1.0 / lon_count)
    cosine = turn_sine(jnp.abs(turns - 0.5) - 0.25)
    shifted = turns + 0.75
    shifted = jnp.where(shifted >= 1.0, shifted - 1.0, shifted)
    sine = turn_sine(jnp.abs(shifted - 0.5) - 0.25)
    return cosine, sine


def fill_table(orders_ref, table_ref, bands, lon_count, degree_total, scale):
    slots = orders_ref.shape[0]
    mine = slots // bands
    shape = (bands, LANES)
    lane = lax.broadcasted_iota(jnp.int32, shape, 1).astype(F32)
    every = orders_ref[...].reshape(1, slots).astype(F32)
    first = mine * lax.broadcasted_iota(jnp.int32, (bands, slots), 0)
    place = lax.broadcasted_iota(jnp.int32, (bands, slots), 1)
    for s in range(mine):
        order = jnp.sum(jnp.where(place == first + s, every, 0.0), 1, keepdims=True)
        order = jnp.broadcast_to(order, shape)
        gain = jnp.where(order < degree_total, scale, 0.0)
        cosine, sine = cosine_sine(order, lane, lon_count)
        cosine, sine = cosine * gain, sine * gain
        turn_c, turn_s = cosine_sine(order, float(LANES), lon_count)
        low = 2 * s * bands
        for start in range(0, lon_count, LANES):
            width = min(LANES, lon_count - start)
            span = slice(start, start + width)
            table_ref[low : low + bands, span] = cosine[:, :width].astype(BF)
            table_ref[low + bands : low + 2 * bands, span] = (-sine[:, :width]).astype(BF)
            cosine, sine = cosine * turn_c - sine * turn_s, sine * turn_c + cosine * turn_s


def send(source, sink, sems, part, width):
    span = pl.ds(part * width, width)
    return pltpu.make_async_copy(source.at[:, :, span], sink.at[:, :, span], sems.at[part])


def analyse_kernel(orders_ref, source_ref, sink_ref, field_ref, out_ref, table, rows, sem, sent, *, bands, degree_total):
    lat, chan, lon = field_ref.shape
    pieces = table.shape[0] // bands
    copy = pltpu.make_async_copy(source_ref, field_ref, sem)
    copy.start()
    fill_table(orders_ref, table, bands, lon, degree_total, 1.0 / math.sqrt(lon))
    copy.wait()
    group = GROUP
    for t0 in range(0, lat, group):
        got = lax.dot_general(
            table[...],
            field_ref[t0 : t0 + group].reshape(group * chan, lon),
            (((1,), (1,)), ((), ())),
            preferred_element_type=F32,
        )
        for u in range(group):
            for start in range(0, pieces, 4):
                line = jnp.concatenate(
                    [
                        got[j * bands : (j + 1) * bands, u * chan : (u + 1) * chan]
                        for j in range(start, start + 4)
                    ],
                    1,
                )
                for q in range(4 * chan // LANES):
                    tile = start * chan // LANES + q
                    rows[tile, pl.ds(t0 + u, bands, lat), :] = line[:, q * LANES : (q + 1) * LANES]
    for q in range(rows.shape[0]):
        packed = rows[q].astype(BF).reshape(out_ref.shape[0], 2, LANES)
        out_ref[:, :, q * LANES : (q + 1) * LANES] = packed
        if q % 3 == 2:
            send(out_ref, sink_ref, sent, q // 3, 3 * LANES).start()
    for g in range(3):
        send(out_ref, sink_ref, sent, g, 3 * LANES).wait()


def analyse(orders, field, bands, degree_total):
    lat, chan, lon = field.shape
    pieces = 2 * orders.shape[0] // bands
    return pl.pallas_call(
        functools.partial(analyse_kernel, bands=bands, degree_total=degree_total),
        in_specs=[VMEM, pl.BlockSpec(memory_space=pl.ANY)],
        out_specs=pl.BlockSpec(memory_space=pl.ANY),
        out_shape=pltpu.HBM((bands * lat // 2, 2, pieces * chan), BF),
        scratch_shapes=[
            pltpu.VMEM(field.shape, BF),
            pltpu.VMEM((bands * lat // 2, 2, pieces * chan), BF),
            pltpu.VMEM((pieces * bands, lon), BF),
            pltpu.VMEM((pieces * chan // LANES, bands * lat, LANES), F32),
            pltpu.SemaphoreType.DMA,
            pltpu.SemaphoreType.DMA((3,)),
        ],
        compiler_params=LIMIT,
        name="analyse",
    )(orders, *off_chip(field))


def tables_kernel(group_ref, a_ref, s_ref, filter_ref, a_out, near_out, s_out, filter_out, sem):
    chan = filter_out.shape[1]
    copy = pltpu.make_async_copy(a_ref, a_out, sem)
    copy.start()
    held = near_out.shape[0]
    for i in range(s_ref.shape[0]):
        turned = s_ref[i].astype(F32).T.astype(BF)
        if i < held:
            near_out[i] = turned
        else:
            s_out[i - held] = turned
    group = group_ref[0]
    kept = filter_ref[:, :chan]
    for g in range(1, filter_ref.shape[1] // chan):
        kept = jnp.where(group == g, filter_ref[:, g * chan : (g + 1) * chan], kept)
    filter_out[...] = kept
    copy.wait()


def tables(group, a, s, filters, chan):
    slots, degrees, lat_all = a.shape
    return pl.pallas_call(
        tables_kernel,
        in_specs=[
            pl.BlockSpec(memory_space=pltpu.SMEM),
            pl.BlockSpec(memory_space=pl.ANY),
            VMEM,
            VMEM,
        ],
        out_specs=[VMEM] * 4,
        out_shape=[
            pltpu.VMEM(a.shape, BF),
            pltpu.VMEM((HELD, lat_all, degrees), BF),
            pltpu.HBM((slots - HELD, lat_all, degrees), BF),
            pltpu.VMEM((degrees, chan), F32),
        ],
        scratch_shapes=[pltpu.SemaphoreType.DMA],
        compiler_params=LIMIT,
        name="tables",
    )(group, *off_chip(a, s, filters))


def scene_kernel(
    group_ref, orders_ref, target_ref, source_ref, table_out, seen_out, field_out, sem, *, bands, degree_total
):
    lat, chan, lon = field_out.shape
    copy = pltpu.make_async_copy(source_ref, field_out, sem)
    copy.start()
    fill_table(orders_ref, table_out, bands, lon, degree_total, 1.0 / math.sqrt(degree_total))
    shape = (chan, target_ref.shape[2])
    place = lax.broadcasted_iota(jnp.int32, shape, 1) - group_ref[0] * chan
    pick = jnp.where(place == lax.broadcasted_iota(jnp.int32, shape, 0), 1.0, 0.0).astype(BF)
    for t in range(lat):
        seen = lax.dot_general(
            pick, target_ref[t], (((1,), (1,)), ((), ())), preferred_element_type=F32
        )
        seen_out[t] = seen.astype(BF)
    copy.wait()


def scene(group, orders, target, field, bands, degree_total):
    _, _, lon = field.shape
    return pl.pallas_call(
        functools.partial(scene_kernel, bands=bands, degree_total=degree_total),
        in_specs=[
            pl.BlockSpec(memory_space=pltpu.SMEM),
            VMEM,
            VMEM,
            pl.BlockSpec(memory_space=pl.ANY),
        ],
        out_specs=[VMEM] * 3,
        out_shape=[
            pltpu.VMEM((2 * orders.shape[0], lon), BF),
            pltpu.HBM(field.shape, BF),
            pltpu.VMEM(field.shape, BF),
        ],
        scratch_shapes=[pltpu.SemaphoreType.DMA],
        compiler_params=LIMIT,
        name="scene",
    )(group, orders, *off_chip(target, field))


def legendre_kernel(
    mine_ref, x_ref, a_ref, near_ref, source_ref, filter_ref, sink_ref, s_ref, out_ref, come, sent
):
    slots, _, lat_all = a_ref.shape
    copies = [
        pltpu.make_async_copy(source_ref.at[i], s_ref.at[i], come.at[i])
        for i in range(s_ref.shape[0])
    ]
    for copy in copies:
        copy.start()
    chan = filter_ref.shape[1]
    degree = lax.broadcasted_iota(jnp.int32, filter_ref.shape, 0)
    scaled = []
    for i in range(slots):
        if i % 2 == 0:
            both = x_ref[:, :, 2 * chan * i : 2 * chan * (i + 2)].reshape(lat_all, 4 * chan)
        x = both[:, 2 * chan * (i % 2) : 2 * chan * (i % 2 + 1)]
        gain = jnp.where(degree >= mine_ref[i], filter_ref[...], 0.0)
        coeffs = jnp.dot(a_ref[i], x, preferred_element_type=F32)
        scaled.append((coeffs * jnp.concatenate([gain, gain], 1)).astype(BF))
    held = near_ref.shape[0]
    for g in range(slots // 2):
        outs = []
        for i in (2 * g, 2 * g + 1):
            if i == held:
                for copy in copies:
                    copy.wait()
            turned = near_ref[i] if i < held else s_ref[i - held]
            outs.append(jnp.dot(turned, scaled[i], preferred_element_type=F32))
        outs = jnp.concatenate(outs, 1).astype(BF).reshape(lat_all // 2, 2, 4 * chan)
        out_ref[:, :, g * 4 * chan : (g + 1) * 4 * chan] = outs
        send(out_ref, sink_ref, sent, g, 4 * chan).start()
    for g in range(slots // 2):
        send(out_ref, sink_ref, sent, g, 4 * chan).wait()


def legendre(mine, x, a, near, s, filters):
    return pl.pallas_call(
        legendre_kernel,
        in_specs=[
            pl.BlockSpec(memory_space=pltpu.SMEM),
            VMEM,
            VMEM,
            VMEM,
            pl.BlockSpec(memory_space=pl.ANY),
            VMEM,
        ],
        out_specs=pl.BlockSpec(memory_space=pl.ANY),
        out_shape=pltpu.HBM(x.shape, BF),
        scratch_shapes=[
            pltpu.VMEM(s.shape, BF),
            pltpu.VMEM(x.shape, BF),
            pltpu.SemaphoreType.DMA((s.shape[0],)),
            pltpu.SemaphoreType.DMA((a.shape[0] // 2,)),
        ],
        compiler_params=LIMIT,
        name="legendre",
    )(mine, *on_chip(x, a, near), *off_chip(s), *on_chip(filters))


def synth_kernel(table_ref, x_ref, field_ref, *rest, places):
    out_ref, part_ref, rows, cols = rest[-4:]
    chan, _ = part_ref.shape[1:]
    bands, _, count, width = x_ref.shape
    pieces = table_ref.shape[0] // bands
    tiles = width // LANES
    for n, place in enumerate(places):
        for q in range(tiles):
            tile = x_ref[:, place, :, q * LANES : (q + 1) * LANES]
            rows[n * tiles + q] = tile.reshape(count * bands, LANES).astype(F32)
        for t in range(count):
            line = [rows[n * tiles + q, pl.ds(t, bands, count), :] for q in range(tiles)]
            line = jnp.concatenate(line, 1).astype(BF)
            at = (n * count + t) * chan
            for j in range(pieces):
                piece = line[:, j * chan : (j + 1) * chan]
                cols[j * bands : (j + 1) * bands, at : at + chan] = piece
    total = lax.dot_general(
        cols[...], table_ref[...], (((0,), (0,)), ((), ())), preferred_element_type=F32
    )
    for t in range(part_ref.shape[0]):
        at = places[0] * count + t
        done = (field_ref[at].astype(F32) + total[t * chan : (t + 1) * chan]).astype(BF)
        out_ref[at] = done
        part_ref[t] = done


def synthesise(table, x, field, places, filled=None):
    _, chan, lon = field.shape
    bands, _, count, width = x.shape
    tiles = width // LANES
    held = count * len(places)
    more = [] if filled is None else [filled]
    return pl.pallas_call(
        functools.partial(synth_kernel, places=places),
        in_specs=[VMEM] * (3 + len(more)),
        out_specs=[VMEM, VMEM],
        out_shape=[pltpu.VMEM(field.shape, BF), pltpu.VMEM((held, chan, lon), BF)],
        input_output_aliases={3: 0} if more else {},
        scratch_shapes=[
            pltpu.VMEM((tiles * len(places), count * bands, LANES), F32),
            pltpu.VMEM((table.shape[0], held * chan), BF),
        ],
        compiler_params=LIMIT,
        name="synthesise",
    )(*on_chip(table, x, field, *more))


def crps_kernel(own_ref, near_ref, far_ref, far_near_ref, seen_ref, *rest, start):
    out_ref, kept_ref = rest[-2:]
    t = pl.program_id(0)
    kept = own_ref[start + t]
    own = kept.astype(F32)

    def slope(other):
        d = own - other.astype(F32)
        return d * lax.rsqrt(d * d + smooth_sq)

    pair = slope(near_ref[start + t]) + slope(far_ref[t]) + slope(far_near_ref[t])
    out_ref[0] = (slope(seen_ref[start + t]) - pair * (1.0 / ENS)).astype(BF)
    kept_ref[0] = kept


def crps(own, near, far, far_near, seen, start, filled=()):
    lat, chan, lon = far.shape
    block = pl.BlockSpec((1, chan, lon), lambda t: (t + start, 0, 0))
    return pl.pallas_call(
        functools.partial(crps_kernel, start=start),
        grid=(lat,),
        in_specs=[VMEM] * 5 + [pl.BlockSpec(memory_space=pl.ANY)] * len(filled),
        out_specs=[block, block],
        out_shape=[jax.ShapeDtypeStruct(own.shape, BF)] * 2,
        input_output_aliases={5: 0, 6: 1} if filled else {},
        compiler_params=LIMIT,
        name="crps",
    )(*on_chip(own, near, far, far_near, seen), *filled)


def body(field, target, slot_orders, analysis, synthesis, degree_filter):
    lat, chan, _ = field.shape[1:]
    mine_count, degrees = analysis.shape[0], analysis.shape[2]
    bands = lax.axis_size("polar")
    ens = lax.axis_size("ens")
    width = 2 * mine_count * chan
    packed = (bands, lat // 2, 2, width)
    flat = (bands * lat // 2, 2, width)
    spectral = analyse(slot_orders, field[0], bands, degrees).reshape(packed)
    got = lax.all_to_all(spectral, "polar", split_axis=0, concat_axis=0, tiled=True)
    group = (lax.axis_index("ens") // ENS).reshape(1)
    mine = lax.dynamic_slice_in_dim(slot_orders, lax.axis_index("polar") * mine_count, mine_count)
    ready = tables(group, jnp.swapaxes(analysis, 1, 2), synthesis, degree_filter.T, chan)
    got, mine, *ready = lax.optimization_barrier((got, mine, *ready))
    out = legendre(mine, got.reshape(flat), *ready)
    back = lax.all_to_all(out.reshape(packed), "polar", split_axis=0, concat_axis=0, tiled=True)
    ready = scene(group, slot_orders, jnp.swapaxes(target, 1, 2), field[0], bands, degrees)
    back, inverse, seen, near_field = lax.optimization_barrier((back, *ready))
    across = [(i, i ^ 2) for i in range(ens)]
    beside = [(i, i ^ 1) for i in range(ens)]
    prediction = None
    fars, starts = [], []
    for places in CHUNKS:
        prediction, part = synthesise(inverse, back, near_field, places, prediction)
        fars.append(lax.ppermute(part, "ens", across))
        starts.append(2 * places[0])
    near = lax.ppermute(prediction, "ens", beside)
    results = ()
    for k, far in enumerate(fars):
        far_near = lax.ppermute(far, "ens", beside)
        results = crps(prediction, near, far, far_near, seen, starts[k], results)
    gradient, prediction = results
    return prediction[None], gradient[None]


def solution(mesh):
    in_specs = (
        P("ens", "polar", None, None),
        P("polar", None, None),
        P(),
        P("polar", None, None),
        P("polar", None, None),
        P(),
    )
    out_specs = (P("ens", "polar", None, None), P("ens", "polar", None, None))
    return jax.shard_map(body, mesh=mesh, in_specs=in_specs, out_specs=out_specs, check_vma=False)
```
